32 devices in a mesh: seq: 4 (over y, x), expert: 8 (over z, core).
Axes of the slice: x: 2, y: 2, z: 4, core: 2. Of those that a mesh axis runs over, the one named last changes fastest.
Arguments:
- tokens: bfloat16 [1024, 7168], P('expert', 'seq'), may hold values from -6 to 6
- cotangent: bfloat16 [1024, 7168], P('expert', 'seq'), may hold values from -6 to 6
- gate_weight: bfloat16 [32, 7168, 1024], P('expert', 'seq'), may hold values from -0.0625 to 0.0625
- up_weight: bfloat16 [32, 7168, 1024], P('expert', 'seq'), may hold values from -0.0625 to 0.0625
- down_weight: bfloat16 [32, 1024, 7168], P('expert', None, 'seq'), may hold values from -0.1875 to 0.1875
- expert_ids: int32 [1024, 8], P('expert'), may hold values from 0 to 31, all different within a row; in each aligned block of 128 rows (0 to 127, 128 to 255, ...) at most 36 rows name the same one
- gate_probs: bfloat16 [1024, 8], P('expert'), may hold values from 0.049804688 to 0.29882812
Outputs:
- token_grad: bfloat16 [1024, 7168], P('expert', 'seq')
- down_grad: bfloat16 [32, 1024, 7168], P('expert', None, 'seq')
The draws below stay inside these ranges and needn't reach their ends.
Inputs may be any that keep to these rules, and one draw needn't show every extreme that they name: `expert_ids`: each token names 8 different experts; among the 128 tokens of one index of expert no expert is named by more than 36 tokens, a bound that some block reaches.
All inputs are finite; a program needn't handle non-finite values.
Results may differ from the reference program's by a relative error of at most 0.018.
Values may be sent and summed in bfloat16 or wider, within the bound.
A program may use at most 192 MiB of HBM per device.

```python
import math
import jax
import jax.numpy as jnp
import numpy as np
from jax import lax

D = 7168
H = 1024
TOPK = 8
EXPERTS = 32
TOK_COL = 128
CAP = 36
TOKENS = 1024
N_SEQ = 4
N_EXPERT = 8


def levels(own_key, extent, cuts, low, top_value):
    factor_of = 1.0
    for position, parts in cuts:
        steps = jax.random.uniform(jax.random.fold_in(jax.random.fold_in(own_key, 6), position), (parts,), jnp.float32, low / len(cuts), top_value / len(cuts))
        factor_of = factor_of * jnp.repeat(jnp.exp(steps), extent[position] // parts).reshape((-1,) + (1,) * (len(extent) - 1 - position))
    return factor_of


def assign_block(key, own, number, rows, count, top, limit, skew):
    ranking = jax.random.permutation(key, count)
    packed, usual = shares(count, rows * top, limit, skew, True), shares(count, rows * top, limit, skew, False)
    places = jnp.arange(count)

    def named(sizes, offset_by):
        used = int((sizes > 0).sum())
        fixed = max(1, used // 4)
        shifted = fixed + (places - fixed + offset_by * (used - fixed)) % max(1, count - fixed)
        return jnp.zeros((count,), jnp.int32).at[ranking[jnp.where(places < fixed, places, shifted)]].set(jnp.asarray(sizes, jnp.int32))

    sizes = jnp.where(number % 4 == 0, named(packed, number // 4), named(usual, number - number // 4 - 1))
    mixed = jax.random.permutation(jax.random.fold_in(own, 3), count)
    giver, receiver = mixed[0:count // 2 * 2:2], mixed[1:count // 2 * 2:2]
    margin = jnp.minimum(sizes[giver] - 1, limit - sizes[receiver]) // 2
    margin = jnp.where((giver == ranking[0]) | (receiver == ranking[0]) | (sizes[receiver] == 0), 0, jnp.maximum(margin, 0))
    shifted = jax.random.randint(jax.random.fold_in(own, 4), (count // 2,), 0, 1 << 20) % (margin + 1)
    sizes = sizes.at[giver].add(-shifted).at[receiver].add(shifted)
    members = jnp.searchsorted(jnp.cumsum(sizes), jnp.arange(rows * top), side="right").astype(jnp.int32)
    grid = members.reshape(top, rows).T
    grid = grid[jax.random.permutation(jax.random.fold_in(own, 1), rows)]
    offset_by = jax.random.randint(jax.random.fold_in(own, 2), (rows, 1), 0, top)
    return jnp.take_along_axis(grid, (jnp.arange(top)[None, :] + offset_by) % top, axis=1)


def shares(number_of, total, most, slope, full):
    portions = [(1 << 20) // math.isqrt(standing ** slope) + 1 for standing in range(1, number_of + 1)]
    largest = most if full else min(most, max(-(-total // number_of), total * portions[0] // sum(portions)))
    least = 1 if total - largest >= number_of - 1 else 0
    given, spare = [largest] + [least] * (number_of - 1), total - largest - least * (number_of - 1)
    while spare > 0:
        candidates = [i for i in range(1, number_of) if given[i] < largest] or [i for i in range(1, number_of) if given[i] < most]
        mass, budget = sum([portions[i] for i in candidates]), spare
        for i in candidates:
            extra = min(most - given[i], max(1, budget * portions[i] // mass), spare)
            given[i] = given[i] + extra
            spare = spare - extra
    return np.array(given)


def centred(rng, dims, scale, limit, split=(), kind=jnp.bfloat16):
    loudness = levels(rng, dims, split, -0.22, 0.18) if split else 1.0
    result = jax.random.normal(rng, dims, jnp.float32) * scale * loudness
    return jnp.minimum(jnp.maximum(result, -limit), limit).astype(kind)


def setup_inputs(seed: int = 0) -> dict:
    streams_of = jax.random.split(jax.random.key(seed), 8)
    tokens = centred(streams_of[0], (TOKENS, D), 1.0, 6.0, ((0, 8), (1, 4)))
    cotangent = centred(streams_of[1], (TOKENS, D), 1.0, 6.0, ((0, 8), (1, 4)))
    gate_weight = centred(streams_of[2], (EXPERTS, D, H), D ** -0.5, 0.0625, ((0, 8), (1, 4)))
    up_weight = centred(streams_of[3], (EXPERTS, D, H), D ** -0.5, 0.0625, ((0, 8), (1, 4)))
    down_weight = centred(streams_of[4], (EXPERTS, H, D), H ** -0.5, 0.1875, ((0, 8), (2, 4)))
    expert_ids_keys = jax.random.split(jax.random.fold_in(streams_of[5], 1), TOKENS // TOK_COL)
    expert_ids_turns = jax.random.permutation(jax.random.fold_in(streams_of[5], 3), TOKENS // TOK_COL)
    expert_ids = jax.vmap(lambda own, number: assign_block(jax.random.fold_in(streams_of[5], 2), own, number, TOK_COL, EXPERTS, TOPK, CAP, 2))(expert_ids_keys, expert_ids_turns).reshape((TOKENS, TOPK))
    gate_probs = jnp.clip(0.049804688 + 0.24902344 * jax.random.uniform(streams_of[6], (TOKENS, TOPK), jnp.float32) ** levels(streams_of[6], (TOKENS, TOPK), ((0, 8),), -0.2, 0.2), 0.049804688, 0.29882812).astype(jnp.bfloat16)
    return {"tokens": tokens, "cotangent": cotangent, "gate_weight": gate_weight, "up_weight": up_weight, "down_weight": down_weight, "expert_ids": expert_ids, "gate_probs": gate_probs}


def slice_sums(pieces):
    rounded = lax.optimization_barrier(pieces.astype(jnp.bfloat16))
    return jnp.sum(rounded.astype(jnp.float32), axis=0)


def reference(tokens, cotangent, gate_weight, up_weight, down_weight, expert_ids, gate_probs):
    row_total = N_EXPERT * CAP
    width = D // N_SEQ
    probs_wide = gate_probs.astype(jnp.float32)

    def per_expert(carry, expert):
        chosen = expert_ids == expert
        routed = jnp.any(chosen, axis=1)
        route_tok = jnp.sum(jnp.where(chosen, probs_wide, 0.0), axis=1)
        sort_key = jnp.where(routed, 0, 1).astype(jnp.int32)
        order = jnp.argsort(sort_key, stable=True)[:row_total].astype(jnp.int32)
        valid = routed[order]
        rows_in = jnp.where(valid[:, None], tokens[order], jnp.zeros((), jnp.bfloat16))
        rows_grad = jnp.where(valid[:, None], cotangent[order], jnp.zeros((), jnp.bfloat16))
        scale = jnp.where(valid, route_tok[order], 0.0)[:, None]
        gate_mat = lax.dynamic_index_in_dim(gate_weight, expert, 0, keepdims=False)
        up_mat = lax.dynamic_index_in_dim(up_weight, expert, 0, keepdims=False)
        down_mat = lax.dynamic_index_in_dim(down_weight, expert, 0, keepdims=False)
        split_in = rows_in.astype(jnp.float32).reshape(row_total, N_SEQ, width)
        split_grad = rows_grad.astype(jnp.float32).reshape(row_total, N_SEQ, width)
        gate_split = gate_mat.astype(jnp.float32).reshape(N_SEQ, width, H)
        up_split = up_mat.astype(jnp.float32).reshape(N_SEQ, width, H)
        down_split = down_mat.astype(jnp.float32).reshape(H, N_SEQ, width)
        highest = lax.Precision.HIGHEST
        pre_gate = slice_sums(jnp.einsum('rnd,ndh->nrh', split_in, gate_split, precision=highest))
        pre_up = slice_sums(jnp.einsum('rnd,ndh->nrh', split_in, up_split, precision=highest))
        back = scale * slice_sums(jnp.einsum('rnd,hnd->nrh', split_grad, down_split, precision=highest))
        sigma = jax.nn.sigmoid(pre_gate)
        weighted = (scale * (pre_gate * sigma * pre_up)).astype(jnp.bfloat16)
        down_part = jnp.dot(weighted.T, rows_grad, preferred_element_type=jnp.float32).astype(jnp.bfloat16)
        up_term = (back * pre_gate * sigma).astype(jnp.bfloat16)
        gate_term = (back * pre_up * sigma * (1.0 + pre_gate * (1.0 - sigma))).astype(jnp.bfloat16)
        assign = jnp.dot(gate_term, gate_mat.T, preferred_element_type=jnp.float32)
        assign = (assign + jnp.dot(up_term, up_mat.T, preferred_element_type=jnp.float32)).astype(jnp.bfloat16)
        contrib = jnp.where(valid[:, None], assign.astype(jnp.float32), 0.0)
        carry = carry.at[order].add(contrib)
        return carry, down_part

    start = jnp.zeros((TOKENS, D), jnp.float32)
    total, down_grad = lax.scan(per_expert, start, jnp.arange(EXPERTS, dtype=jnp.int32))
    return total.astype(jnp.bfloat16), down_grad
```

```python
import jax
import jax.numpy as jnp
from jax import lax
from jax.sharding import PartitionSpec as P

CAP = 36
GROUPS = 2


def gating(pre_gate, pre_up, back_sum, scale):
    sigma = jax.nn.sigmoid(pre_gate)
    back = scale * back_sum
    weighted = (scale * (pre_gate * sigma * pre_up)).astype(jnp.bfloat16)
    up_term = (back * pre_gate * sigma).astype(jnp.bfloat16)
    gate_term = (back * pre_up * sigma * (1.0 + pre_gate * (1.0 - sigma))).astype(jnp.bfloat16)
    return (weighted, gate_term, up_term)


def contract_rows(left, right):
    return lax.dot_general(
        left, right, (((1,), (1,)), ((), ())), preferred_element_type=jnp.float32
    )


def exchange(block, bit):
    size = lax.axis_size("seq")
    return lax.ppermute(block, "seq", [(i, i ^ bit) for i in range(size)])


def seq_bit(bit):
    return (lax.axis_index("seq") // bit) % 2


def scatter_first(block):
    half = block.shape[1] // 2
    quarter = half // 2
    halves = []
    for start, bits in ((0, (1, 2)), (half, (2, 1))):
        side = seq_bit(bits[0])
        kept = lax.dynamic_slice_in_dim(block, start + side * quarter, quarter, 1)
        sent = lax.dynamic_slice_in_dim(block, start + (1 - side) * quarter, quarter, 1)
        halves.append((kept, exchange(sent, bits[0])))
    return halves


def scatter_second(halves):
    out = []
    for (kept, came), bit in zip(halves, (2, 1)):
        side = seq_bit(bit)
        eighth = kept.shape[1] // 2
        total = (kept.astype(jnp.float32) + came.astype(jnp.float32)).astype(jnp.bfloat16)
        mine = lax.dynamic_slice_in_dim(total, side * eighth, eighth, 1)
        other = lax.dynamic_slice_in_dim(total, (1 - side) * eighth, eighth, 1)
        out.append((mine, exchange(other, bit)))
    return out


def scatter_last(parts):
    return [mine.astype(jnp.float32) + came.astype(jnp.float32) for mine, came in parts]


def after(value, *done):
    return lax.optimization_barrier((value,) + done)[0]


def paired(own, came, bit):
    first = seq_bit(bit) == 0
    return jnp.concatenate([jnp.where(first, own, came), jnp.where(first, came, own)], axis=1)


def body(tokens, cotangent, gate_weight, up_weight, down_weight, expert_ids, gate_probs):
    here = gate_weight.shape[0]
    sources = lax.axis_size("expert")
    tok_count = tokens.shape[0]
    top = expert_ids.shape[1]
    total = sources * tok_count
    rows = sources * CAP
    meta = jnp.concatenate(
        [expert_ids.astype(jnp.float32), gate_probs.astype(jnp.float32)], axis=1
    )
    meta_all = lax.all_gather(meta, "expert", axis=0, tiled=True)
    tokens_all = lax.all_gather(tokens, "expert", axis=0, tiled=True)
    cotangent_all = lax.all_gather(cotangent, "expert", axis=0, tiled=True)

    ids = meta_all[:, :top].T
    probs = meta_all[:, top:].T
    mine = (lax.axis_index("expert") * here + jnp.arange(here, dtype=jnp.int32)).astype(jnp.float32)
    named = ids[None, :, :] == mine[:, None, None]
    chosen = jnp.any(named, axis=1)
    route = jnp.sum(jnp.where(named, probs[None], 0.0), axis=1)
    before = (
        jnp.arange(tok_count)[:, None] < jnp.arange(tok_count)[None, :]
    ).astype(jnp.bfloat16)
    rank = jnp.dot(
        chosen.astype(jnp.bfloat16).reshape(here * sources, tok_count),
        before,
        preferred_element_type=jnp.float32,
    ).reshape(here, sources, tok_count).astype(jnp.int32)
    slot = rank + CAP * jnp.arange(sources, dtype=jnp.int32)[None, :, None]
    slot = jnp.where(chosen, slot.reshape(here, total), -1)
    hits = slot[:, None, :] == jnp.arange(rows, dtype=jnp.int32)[None, :, None]
    pick = hits.astype(jnp.bfloat16)
    scale = jnp.sum(jnp.where(hits, route[:, None, :], 0.0), axis=2)[:, :, None]

    def rows_of(e, source):
        return jnp.dot(pick[e], source, preferred_element_type=jnp.float32).astype(jnp.bfloat16)

    groups = GROUPS if here % GROUPS == 0 else 1
    per = here // groups
    spans = [range(g * per, (g + 1) * per) for g in range(groups)]
    first_gu = []
    for g, span in enumerate(spans):
        with jax.named_scope(f"gu{g}"):
            gates, ups = [], []
            for e in span:
                x = rows_of(e, tokens_all)
                if g and e == span[-1]:
                    x = after(x, *[came for _, came in first_gu[-1]])
                gates.append(jnp.dot(x, gate_weight[e], preferred_element_type=jnp.float32).astype(jnp.bfloat16))
                ups.append(jnp.dot(x, up_weight[e], preferred_element_type=jnp.float32).astype(jnp.bfloat16))
            first_gu.append(scatter_first(jnp.concatenate(gates + ups, axis=0)))
    second_gu = [scatter_second(halves) for halves in first_gu]
    cotangent_all = after(cotangent_all, *[came for _, came in first_gu[-1]])
    if groups > 1:
        cotangent_all = after(cotangent_all, *[came for _, came in second_gu[0]])
    grads = []
    first_b = []
    for g, span in enumerate(spans):
        with jax.named_scope(f"back{g}"):
            parts = []
            for e in span:
                y = rows_of(e, cotangent_all)
                if g and e == span[-1]:
                    y = after(y, *[came for _, came in first_b[-1]])
                grads.append(y)
                parts.append(contract_rows(y, down_weight[e]).astype(jnp.bfloat16))
            first_b.append(scatter_first(jnp.concatenate(parts, axis=0)))
    down_parts = []
    pieces = []
    for g, span in enumerate(spans):
        with jax.named_scope(f"terms{g}"):
            summed_gu = scatter_last(second_gu[g])
            summed_b = scatter_last(scatter_second(first_b[g]))
            scale_g = scale[g * per : (g + 1) * per].reshape(per * rows, 1)
            owned = []
            for gu, back in zip(summed_gu, summed_b):
                owned.append(
                    jnp.concatenate(gating(gu[: per * rows], gu[per * rows :], back, scale_g), axis=0)
                )
            wide = [paired(part, exchange(part, bit), bit) for part, bit in zip(owned, (2, 1))]
            came = [exchange(part, bit) for part, bit in zip(wide, (1, 2))]
            if g:
                came = [after(block, *pieces) for block in came]
            full = [paired(part, block, bit) for part, block, bit in zip(wide, came, (1, 2))]
            terms = jnp.concatenate(full, axis=1).reshape(3, per, rows, -1)
        for i, e in enumerate(span):
            piece = contract_rows(terms[1, i], gate_weight[e])
            piece = piece + contract_rows(terms[2, i], up_weight[e])
            pieces.append(piece.astype(jnp.bfloat16))
        for i, e in enumerate(span):
            down_part = lax.dot_general(
                terms[0, i], grads[e], (((0,), (0,)), ((), ())), preferred_element_type=jnp.float32
            )
            down_parts.append(down_part.astype(jnp.bfloat16))
    down_grad = jnp.stack(down_parts, axis=0)
    partial = lax.dot_general(
        pick.reshape(here * rows, total),
        jnp.concatenate(pieces, axis=0),
        (((0,), (0,)), ((), ())),
        preferred_element_type=jnp.float32,
    ).astype(jnp.bfloat16)
    token_grad = lax.psum_scatter(partial, "expert", scatter_dimension=0, tiled=True)
    return (token_grad, down_grad)


def solution(mesh):
    in_specs = (
        P("expert", "seq"),
        P("expert", "seq"),
        P("expert", "seq", None),
        P("expert", "seq", None),
        P("expert", None, "seq"),
        P("expert", None),
        P("expert", None),
    )
    out_specs = (P("expert", "seq"), P("expert", None, "seq"))
    return jax.shard_map(body, mesh=mesh, in_specs=in_specs, out_specs=out_specs, check_vma=False)
```
